128 devices in a mesh: dom: 8 (over z, core), grp: 16 (over x, y).
Axes of the slice: x: 4, y: 4, z: 4, core: 2. Of those that a mesh axis runs over, the one named last changes fastest.
Arguments:
- src_table: float32 [16384, 400], P(('dom', 'grp')), may hold values from -8 to 8
- src_state: float32 [16384], P(('dom', 'grp')), may hold values from 0.01 to 1
- tgt_table: float32 [131072, 400], P(('dom', 'grp')), may hold values from -8 to 8
- tgt_state: float32 [131072], P(('dom', 'grp')), may hold values from 0.01 to 1
- pair_source: int32 [2, 131072], P(None, ('dom', 'grp')), may hold values from 0 to 127
- pair_owner: int32 [2, 131072, 1], P(None, ('dom', 'grp')), may hold values from 0 to 15; in each aligned block of 1024 rows (0 to 1023, 1024 to 2047, ..., all dimensions but the last counted through in order) at most 256 rows name the same one
- pair_offset: int32 [2, 131072], P(None, ('dom', 'grp')), may hold values from 0 to 1023
- negatives: int32 [8, 1000], P('dom'), may hold values from 0 to 16383
- plan: int32 [2, 8], replicated, may hold values from 0 to 7, each once within a row
Outputs:
- src_trained: float32 [16384, 400], P(('dom', 'grp'))
- src_accum: float32 [16384], P(('dom', 'grp'))
- tgt_trained: float32 [131072, 400], P(('dom', 'grp'))
- tgt_accum: float32 [131072], P(('dom', 'grp'))
The draws below stay inside these ranges and needn't reach their ends.
Inputs may be any that keep to these rules, and one draw needn't show every extreme that they name: `pair_owner`: in every round the pairs of one device name each owner at most 256 times, and some device's pairs name some owner exactly 256 times. `plan`: each round's row names every dom index once.
All inputs are finite; a program needn't handle non-finite values.
Results may differ from the reference program's by a relative error of at most 0.011.
Values may be sent and summed in bfloat16 or wider, within the bound.
No kernel may reach another device: no remote copies, remote signals or barrier semaphores. Data moves between devices by JAX's collectives and lax.ppermute only.
A program may use at most 128 MiB of HBM per device.

```python
import math
import jax
import jax.numpy as jnp
import numpy as np
from jax import lax

D = 400
NEG = 1000
ROUNDS = 2
SRC_DEV = 128
TGT_DEV = 1024
PAIR_DEV = 1024
CAP = 256
PAIRS = 131072
SRC_ROWS = 16384
TGT_ROWS = 131072
N_DOM = 8
N_GRP = 16


def table_values(key, row_total):
    return jnp.clip(0.4 * jax.random.normal(key, (row_total, D), jnp.float32), -2.4, 2.4)


def draw_src_table(key, part):
    return table_values(jax.random.fold_in(key, 11), SRC_ROWS)


def draw_tgt_table(key, part):
    return table_values(jax.random.fold_in(key, 23), TGT_ROWS)


def plant(result, stream_key, least, high):
    longest = result.shape.index(max(result.shape))
    spots = []
    for shift in (0, 1):
        where = [jax.random.randint(jax.random.fold_in(stream_key, axis), (), 0, length) for axis, length in enumerate(result.shape)]
        where[longest] = (where[longest] + shift) % result.shape[longest]
        spots.append(tuple(where))
    return result.at[spots[0]].set(least).at[spots[1]].set(high)


def steps_of(key, dims, pieces, least, top_value):
    loudness, own = 1.0, jax.random.fold_in(key, 6)
    for dim, shards_of in pieces:
        draws = jnp.exp(jax.random.uniform(jax.random.fold_in(own, dim), (shards_of,), jnp.float32, least / len(pieces), top_value / len(pieces)))
        loudness = loudness * jnp.repeat(draws, dims[dim] // shards_of).reshape([-1 if axis == dim else 1 for axis in range(len(dims))])
    return loudness


def deal_out(key, own, number, rows, count, top, bound, lean):
    ranking = jax.random.permutation(key, count)
    packed, usual = load_shares(count, rows * top, bound, lean, True), load_shares(count, rows * top, bound, lean, False)
    places = jnp.arange(count)

    def named(tallies, rotation):
        used = int((tallies > 0).sum())
        fixed = max(1, used // 4)
        moved = fixed + (places - fixed + rotation * (used - fixed)) % max(1, count - fixed)
        return jnp.zeros((count,), jnp.int32).at[ranking[jnp.where(places < fixed, places, moved)]].set(jnp.asarray(tallies, jnp.int32))

    tallies = jnp.where(number % 4 == 0, named(packed, number // 4), named(usual, number - number // 4 - 1))
    mixed = jax.random.permutation(jax.random.fold_in(own, 3), count)
    donor, taker = mixed[0:count // 2 * 2:2], mixed[1:count // 2 * 2:2]
    margin = jnp.minimum(tallies[donor] - 1, bound - tallies[taker]) // 2
    margin = jnp.where((donor == ranking[0]) | (taker == ranking[0]) | (tallies[taker] == 0), 0, jnp.maximum(margin, 0))
    moved = jax.random.randint(jax.random.fold_in(own, 4), (count // 2,), 0, 1 << 20) % (margin + 1)
    tallies = tallies.at[donor].add(-moved).at[taker].add(moved)
    labels = jnp.searchsorted(jnp.cumsum(tallies), jnp.arange(rows * top), side="right").astype(jnp.int32)
    listing = labels.reshape(top, rows).T
    listing = listing[jax.random.permutation(jax.random.fold_in(own, 1), rows)]
    rotation = jax.random.randint(jax.random.fold_in(own, 2), (rows, 1), 0, top)
    return jnp.take_along_axis(listing, (jnp.arange(top)[None, :] + rotation) % top, axis=1)


def load_shares(number_of, total, most, skew, full):
    portions = [(1 << 20) // math.isqrt(grade ** skew) + 1 for grade in range(1, number_of + 1)]
    largest = most if full else min(most, max(-(-total // number_of), total * portions[0] // sum(portions)))
    least = 1 if total - largest >= number_of - 1 else 0
    holding, rest = [largest] + [least] * (number_of - 1), total - largest - least * (number_of - 1)
    while rest > 0:
        movable = [i for i in range(1, number_of) if holding[i] < largest] or [i for i in range(1, number_of) if holding[i] < most]
        whole, left = sum([portions[i] for i in movable]), rest
        for i in movable:
            addition = min(most - holding[i], max(1, left * portions[i] // whole), rest)
            holding[i] = holding[i] + addition
            rest = rest - addition
    return np.array(holding)


def setup_inputs(seed: int = 0) -> dict:
    key_list = jax.random.split(jax.random.key(seed), 10)
    src_table = draw_src_table(jax.random.fold_in(key_list[9], 71), 0)
    src_state = jnp.clip(jnp.exp(math.log(1.0) - 4.6051702 * jax.random.uniform(key_list[1], (SRC_ROWS,), jnp.float32) ** steps_of(key_list[1], (SRC_ROWS,), ((0, 128),), -0.2, 0.2)), 0.01, 1.0)
    tgt_table = draw_tgt_table(jax.random.fold_in(key_list[9], 71), 0)
    tgt_state = jnp.clip(jnp.exp(math.log(1.0) - 4.6051702 * jax.random.uniform(key_list[3], (TGT_ROWS,), jnp.float32) ** steps_of(key_list[3], (TGT_ROWS,), ((0, 128),), -0.2, 0.2)), 0.01, 1.0)
    pair_source = plant(jax.random.randint(key_list[4], (ROUNDS, PAIRS), 0, SRC_DEV), jax.random.fold_in(key_list[4], 1), 0, SRC_DEV - 1).astype(jnp.int32)
    pair_owner_keys = jax.random.split(jax.random.fold_in(key_list[5], 1), ROUNDS * PAIRS // PAIR_DEV)
    pair_owner_turns = jax.random.permutation(jax.random.fold_in(key_list[5], 3), ROUNDS * PAIRS // PAIR_DEV)
    pair_owner = jax.vmap(lambda own, number: deal_out(jax.random.fold_in(key_list[5], 2), own, number, PAIR_DEV, N_GRP, 1, CAP, 2))(pair_owner_keys, pair_owner_turns).reshape((ROUNDS, PAIRS, 1))
    pair_offset = plant(jax.random.randint(key_list[6], (ROUNDS, PAIRS), 0, TGT_DEV), jax.random.fold_in(key_list[6], 1), 0, TGT_DEV - 1).astype(jnp.int32)
    negatives = plant(jax.random.randint(key_list[7], (N_DOM, NEG), 0, N_GRP * TGT_DEV), jax.random.fold_in(key_list[7], 1), 0, (N_GRP * TGT_DEV) - 1).astype(jnp.int32)
    plan = jax.vmap(lambda own: jax.random.permutation(own, N_DOM))(jax.random.split(key_list[8], ROUNDS)).reshape((ROUNDS, N_DOM)).astype(jnp.int32)
    return dict(src_table=src_table, src_state=src_state, tgt_table=tgt_table, tgt_state=tgt_state, pair_source=pair_source, pair_owner=pair_owner, pair_offset=pair_offset, negatives=negatives, plan=plan)


LEARN = 0.1

def adagrad(emb_table, opt_state, grads):
    new_state = opt_state + lax.optimization_barrier(jnp.mean(grads * grads, axis=1))
    return (emb_table - LEARN * grads / jnp.sqrt(new_state)[:, None], new_state)

def reference(src_table, src_state, tgt_table, tgt_state, pair_source, pair_owner, pair_offset, negatives, plan):
    src_part_rows = N_GRP * SRC_DEV
    tgt_part_rows = N_GRP * TGT_DEV
    group_pairs = N_GRP * PAIR_DEV
    src_parts = src_table.reshape(N_DOM, src_part_rows, D)
    src_states = src_state.reshape(N_DOM, src_part_rows)
    tgt_parts = tgt_table.reshape(N_DOM, tgt_part_rows, D)
    tgt_states = tgt_state.reshape(N_DOM, tgt_part_rows)
    device_of_pair = (jnp.arange(group_pairs, dtype=jnp.int32) // PAIR_DEV).astype(jnp.int32)
    for round_index in range(ROUNDS):
        new_src, new_src_state = (src_parts, src_states)
        new_tgt, new_tgt_state = (tgt_parts, tgt_states)
        for domain in range(N_DOM):
            partition = plan[round_index, domain]
            begin = domain * group_pairs
            source_ids = device_of_pair * SRC_DEV + pair_source[round_index, begin:begin + group_pairs]
            target_ids = pair_owner[round_index, begin:begin + group_pairs, 0] * TGT_DEV + pair_offset[round_index, begin:begin + group_pairs]
            source_emb = src_parts[partition]
            target_emb = tgt_parts[domain]
            source_rows = source_emb[source_ids].astype(jnp.bfloat16)
            target_rows = target_emb[target_ids].astype(jnp.bfloat16)
            negative_rows = target_emb[negatives[domain]].astype(jnp.bfloat16)
            positive = lax.optimization_barrier(jnp.sum(source_rows.astype(jnp.float32) * target_rows.astype(jnp.float32), axis=1))
            negative = jnp.dot(source_rows, negative_rows.T, preferred_element_type=jnp.float32)
            score_max = jnp.maximum(lax.optimization_barrier(jnp.max(negative, axis=1)), positive)
            pos_exp = jnp.exp(positive - score_max)
            neg_exp = jnp.exp(negative - score_max[:, None])
            exp_total = pos_exp + lax.optimization_barrier(jnp.sum(neg_exp, axis=1))
            d_pos = pos_exp / exp_total - 1.0
            d_neg = (neg_exp / exp_total[:, None]).astype(jnp.bfloat16)
            source_grad = (d_pos[:, None] * target_rows.astype(jnp.float32) + jnp.dot(d_neg, negative_rows, preferred_element_type=jnp.float32)).astype(jnp.bfloat16)
            src_grads = jnp.zeros((src_part_rows, D), jnp.float32).at[source_ids].add(source_grad.astype(jnp.float32))
            tgt_grads = jnp.zeros((tgt_part_rows, D), jnp.float32).at[target_ids].add(d_pos[:, None] * source_rows.astype(jnp.float32))
            tgt_grads = tgt_grads.at[negatives[domain]].add(jnp.dot(d_neg.T, source_rows, preferred_element_type=jnp.float32))
            src_new, src_state_new = adagrad(source_emb, src_states[partition], src_grads)
            tgt_new, tgt_state_new = adagrad(target_emb, tgt_states[domain], tgt_grads)
            new_src = new_src.at[partition].set(src_new)
            new_src_state = new_src_state.at[partition].set(src_state_new)
            new_tgt = new_tgt.at[domain].set(tgt_new)
            new_tgt_state = new_tgt_state.at[domain].set(tgt_state_new)
        src_parts, src_states = (new_src, new_src_state)
        tgt_parts, tgt_states = (new_tgt, new_tgt_state)
    return (src_parts.reshape(SRC_ROWS, D), src_states.reshape(SRC_ROWS), tgt_parts.reshape(TGT_ROWS, D), tgt_states.reshape(TGT_ROWS))
```

```python
import jax
import jax.numpy as jnp
from jax import lax
from jax.experimental import pallas as pl
from jax.experimental.pallas import tpu as pltpu
from jax.sharding import PartitionSpec as P

LEARN = 0.1
SIDE = 4
BF = jnp.bfloat16
F32 = jnp.float32
BIG = 3.0e38


def shift(value, dx, dy):
    table = [
        (((i // SIDE + dx) % SIDE) * SIDE + (i % SIDE + dy) % SIDE, i) for i in range(SIDE * SIDE)
    ]
    return lax.ppermute(value, "grp", table)


def line_gather(value, axis):
    return [value] + [shift(value, k if axis == 0 else 0, k if axis == 1 else 0) for k in (1, 2, 3)]


def line_scatter(pieces, axis):
    return [pieces[0]] + [
        shift(pieces[k], -k if axis == 0 else 0, -k if axis == 1 else 0) for k in (1, 2, 3)
    ]


def group_gather(block):
    half = block.shape[0] // 2
    first = jnp.concatenate(line_gather(block[:half], 0), axis=0)
    second = jnp.concatenate(line_gather(block[half:], 1), axis=0)
    return line_gather(first, 1) + line_gather(second, 0)


def group_scatter(pieces, add):
    half = pieces[0].shape[0] // SIDE
    first = add(line_scatter(pieces[:SIDE], 1))
    second = add(line_scatter(pieces[SIDE:], 0))
    cut = lambda whole: [whole[k * half : (k + 1) * half] for k in range(SIDE)]
    return line_scatter(cut(first), 0), line_scatter(cut(second), 1)


def add_rounded(parts):
    total = parts[0].astype(F32)
    for part in parts[1:]:
        total = total + part.astype(F32)
    return total.astype(parts[0].dtype)


def add_exact(parts):
    return (parts[0] + parts[1]) + (parts[2] + parts[3])


def group_sum(value):
    for axis in (0, 1):
        parts = line_gather(value, axis)
        value = (parts[0] + parts[1]) + (parts[2] + parts[3])
    return value


def dom_fetch(values, want, my_dom):
    doms = want.shape[0]
    my_z = my_dom // 2
    my_c = my_dom % 2
    swap = [(i, i ^ 1) for i in range(doms)]
    both = [(value, lax.ppermute(value, "dom", swap)) for value in values]

    def choose(dest):
        own = (want[dest] % 2) == my_c
        return [jnp.where(own, pair[0], pair[1]) for pair in both]

    zs = doms // 2
    got = [choose(my_dom)]
    for k in range(1, zs):
        outgoing = choose(((my_z + k) % zs) * 2 + my_c)
        table = [(i, ((i // 2 + k) % zs) * 2 + i % 2) for i in range(doms)]
        got.append([lax.ppermute(value, "dom", table) for value in outgoing])
    from_k = (my_z - want[my_dom] // 2) % zs
    out = []
    for j in range(len(values)):
        value = got[0][j]
        for k in range(1, zs):
            value = jnp.where(from_k == k, got[k][j], value)
        out.append(value)
    return out


def nt(a, b):
    return lax.dot_general(a, b, (((1,), (1,)), ((), ())), preferred_element_type=F32)


def tn(a, b):
    return lax.dot_general(a, b, (((0,), (0,)), ((), ())), preferred_element_type=F32)


VM = pltpu.VMEM
PARAMS = pltpu.CompilerParams(vmem_limit_bytes=56 << 20)


def masked_negatives(table, id_col, base):
    rows, width = table.shape
    count = id_col.shape[0]
    piece = count // 8

    def body(base_ref, table_ref, id_ref, *outs):
        t_bf = table_ref[...].astype(BF)
        for p in range(8):
            ids = id_ref[p * piece : (p + 1) * piece, :] - base_ref[0]
            hot = (ids == lax.broadcasted_iota(jnp.int32, (piece, rows), 1)).astype(F32).astype(BF)
            outs[p][...] = jnp.dot(hot, t_bf, preferred_element_type=F32).astype(BF)

    return pl.pallas_call(
        body,
        name="masked_negatives",
        out_shape=[jax.ShapeDtypeStruct((piece, width), BF)] * 8,
        grid_spec=pltpu.PrefetchScalarGridSpec(
            num_scalar_prefetch=1,
            grid=(1,),
            in_specs=[
                pl.BlockSpec((rows, width), lambda i, s: (0, 0)),
                pl.BlockSpec((count, 1), lambda i, s: (0, 0)),
            ],
            out_specs=[pl.BlockSpec((piece, width), lambda i, s: (0, 0))] * 8,
        ),
        compiler_params=PARAMS,
    )(base, table, id_col)


def pair_counts(meta, base, src_count, tgt_count):
    blocks, _, pairs = meta.shape
    half = src_count // 2

    def body(base_ref, meta_ref, first_ref, second_ref):
        word = meta_ref[0]
        src = word & 127
        code = (word >> 7) - base_ref[0]
        a = (src == lax.broadcasted_iota(jnp.int32, (src_count, pairs), 0)).astype(F32).astype(BF)
        b = (code == lax.broadcasted_iota(jnp.int32, (tgt_count, pairs), 0)).astype(F32).astype(BF)
        number = nt(a, b).astype(BF)
        first_ref[0, 0] = number[:half]
        second_ref[0, 0] = number[half:]

    out = jax.ShapeDtypeStruct((SIDE, SIDE, half, tgt_count), BF)
    return pl.pallas_call(
        body,
        name="pair_counts",
        out_shape=[out, out],
        grid_spec=pltpu.PrefetchScalarGridSpec(
            num_scalar_prefetch=1,
            grid=(SIDE, SIDE),
            in_specs=[pl.BlockSpec((1, 1, pairs), lambda ky, kx, s: (ky * SIDE + kx, 0, 0))],
            out_specs=[
                pl.BlockSpec((1, 1, half, tgt_count), lambda ky, kx, s: (ky, kx, 0, 0)),
                pl.BlockSpec((1, 1, half, tgt_count), lambda ky, kx, s: (kx, ky, 0, 0)),
            ],
        ),
        compiler_params=PARAMS,
    )(base, meta)


def score_round(place, src_pieces, neg_pieces, table, id_row, count_a, count_b):
    rows, width = src_pieces[0].shape
    neg_rows = neg_pieces[0].shape[0]
    negs = neg_rows * 8
    targets = table.shape[0]
    own = rows // SIDE
    count_a = count_a.reshape(SIDE, rows, targets)
    count_b = count_b.reshape(SIDE, rows, targets)

    def body(place_ref, *refs):
        s_in, refs = refs[:8], refs[8:]
        n_in, refs = refs[:8], refs[8:]
        t_ref, id_ref, ca_ref, cb_ref = refs[:4]
        u_out, refs = refs[4:12], refs[12:]
        grad_ref, soft_ref, q_ref, v_ref, src_ref = refs[:5]
        s_buf, n_buf, t_buf, s_sem, n_sem = refs[5:]
        p = pl.program_id(0)

        @pl.when(p == 0)
        def _():
            for k in range(8):
                pltpu.make_async_copy(s_in[k], s_buf.at[k], s_sem.at[k]).start()
                pltpu.make_async_copy(
                    n_in[k], n_buf.at[pl.ds(k * neg_rows, neg_rows)], n_sem.at[k]
                ).start()
            t_buf[...] = t_ref[...].astype(BF)
            grad_ref[...] = jnp.zeros_like(grad_ref)
            for k in range(8):
                pltpu.make_async_copy(
                    n_in[k], n_buf.at[pl.ds(k * neg_rows, neg_rows)], n_sem.at[k]
                ).wait()

        for k in range(8):

            @pl.when(p == k)
            def _():
                pltpu.make_async_copy(s_in[k], s_buf.at[k], s_sem.at[k]).wait()

        s = s_buf[p]
        neg = n_buf[...]
        t = t_buf[...]
        src_ref[0] = s
        out = jnp.where(id_ref[...] < 0, -BIG, 0.0)
        pn = nt(s, neg) + out
        top = jnp.max(pn, axis=1, keepdims=True)
        en = jnp.exp(pn - top)
        total = jnp.sum(en, axis=1, keepdims=True)

        for k in (0, SIDE):

            @pl.when(p == k)
            def _():
                mix = jnp.dot(en[:own].astype(BF), neg, preferred_element_type=F32)
                v_ref[k // SIDE] = mix / total[:own]

        d = nt(s, t) - top
        x = jnp.exp(-jnp.abs(d))
        above = d > 0
        e1 = jnp.where(above, 1.0, x)
        e2 = total * jnp.where(above, x, 1.0)
        q = e2 / (e1 + e2)
        number = jnp.where(p < SIDE, ca_ref[0], cb_ref[0]).astype(F32)
        nq = (number * q).astype(BF)
        soft_ref[0] = (e1 * (1.0 / total)).astype(BF)
        u = jnp.dot(nq, t, preferred_element_type=F32).astype(BF)
        for k in range(8):

            @pl.when(p == k)
            def _():
                u_out[k][...] = u

        grad_ref[...] += tn(nq, s)
        q_row = nt(jnp.ones((8, targets), BF), nq)
        turn = jnp.where(p < SIDE, place_ref[0], place_ref[1])
        line = jnp.where(p < SIDE, place_ref[1], place_ref[0])
        spot = (p + line) % SIDE + jnp.where(p < SIDE, 0, SIDE)
        q_ref[pl.ds(spot, 1), :] = pltpu.roll(q_row, turn * own, 1)[0:1]

    any_spec = pl.BlockSpec(memory_space=pl.ANY)
    full = lambda shape: pl.BlockSpec(shape, lambda i, s: (0,) * len(shape))
    outs = pl.pallas_call(
        body,
        name="score_round",
        out_shape=[jax.ShapeDtypeStruct((rows, width), BF)] * 8
        + [
            jax.ShapeDtypeStruct((targets, width), F32),
            jax.ShapeDtypeStruct((8, rows, targets), BF),
            jax.ShapeDtypeStruct((8, rows), F32),
            jax.ShapeDtypeStruct((2, own, width), F32),
            jax.ShapeDtypeStruct((8, rows, width), BF),
        ],
        grid_spec=pltpu.PrefetchScalarGridSpec(
            num_scalar_prefetch=1,
            grid=(8,),
            in_specs=[any_spec] * 16
            + [
                full((targets, width)),
                full((1, negs)),
                pl.BlockSpec((1, rows, targets), lambda i, s: (jnp.minimum(i, SIDE - 1), 0, 0)),
                pl.BlockSpec((1, rows, targets), lambda i, s: (jnp.maximum(i - SIDE, 0), 0, 0)),
            ],
            out_specs=[full((rows, width))] * 8
            + [
                full((targets, width)),
                pl.BlockSpec((1, rows, targets), lambda i, s: (i, 0, 0)),
                full((8, rows)),
                full((2, own, width)),
                pl.BlockSpec((1, rows, width), lambda i, s: (i, 0, 0)),
            ],
            scratch_shapes=[
                VM((8, rows, width), BF),
                VM((negs, width), BF),
                VM((targets, width), BF),
                pltpu.SemaphoreType.DMA((8,)),
                pltpu.SemaphoreType.DMA((8,)),
            ],
        ),
        compiler_params=PARAMS,
    )(place, *src_pieces, *neg_pieces, table, id_row, count_a, count_b)
    return outs[:8], outs[8:]


def target_update(place, grad, soft, q_all, src_all, id_row, table, state):
    targets, width = table.shape
    rows = src_all.shape[1]
    negs = id_row.shape[1]
    own = rows // SIDE

    def body(place_ref, grad_ref, soft_ref, q_ref, s_ref, id_ref, t_ref, st_ref, new_ref, nst_ref, acc):
        p = pl.program_id(0)

        @pl.when(p == 0)
        def _():
            acc[...] = jnp.zeros_like(acc)

        turn = jnp.where(p < SIDE, place_ref[0], place_ref[1])
        line = jnp.where(p < SIDE, place_ref[1], place_ref[0])
        spot = (p + line) % SIDE + jnp.where(p < SIDE, 0, SIDE)
        row = jnp.broadcast_to(q_ref[pl.ds(spot, 1), :], (8, rows))
        row = pltpu.roll(row, ((SIDE - turn) % SIDE) * own, 1)
        weight = row.T[:, 0:1]
        scaled = (s_ref[0].astype(F32) * weight).astype(BF)
        acc[...] += tn(soft_ref[0], scaled)

        @pl.when(p == 7)
        def _():
            mine = lax.broadcasted_iota(jnp.int32, (targets, negs), 0) + place_ref[2]
            times = jnp.sum((id_ref[...] == mine).astype(F32), axis=1, keepdims=True)
            g = times * acc[...] - grad_ref[...]
            st = st_ref[...] + jnp.sum(g * g, axis=1, keepdims=True) * (1.0 / width)
            nst_ref[...] = st
            new_ref[...] = t_ref[...] - LEARN * g / jnp.sqrt(st)

    full = lambda shape: pl.BlockSpec(shape, lambda i, s: (0,) * len(shape))
    return pl.pallas_call(
        body,
        name="target_update",
        out_shape=[
            jax.ShapeDtypeStruct((targets, width), F32),
            jax.ShapeDtypeStruct((targets, 1), F32),
        ],
        grid_spec=pltpu.PrefetchScalarGridSpec(
            num_scalar_prefetch=1,
            grid=(8,),
            in_specs=[
                full((targets, width)),
                pl.BlockSpec((1, rows, targets), lambda i, s: (i, 0, 0)),
                full((8, rows)),
                pl.BlockSpec((1, rows, width), lambda i, s: (i, 0, 0)),
                full((1, negs)),
                full((targets, width)),
                full((targets, 1)),
            ],
            out_specs=[full((targets, width)), full((targets, 1))],
            scratch_shapes=[VM((targets, width), F32)],
        ),
        compiler_params=PARAMS,
    )(place, grad, soft, q_all, src_all, id_row, table, state)


def source_update(place, parts_a, parts_b, q_all, mix, table, state):
    count, width = table.shape
    half = count // 2
    rows = q_all.shape[1]

    def body(place_ref, *refs):
        a_in, b_in = refs[:SIDE], refs[SIDE : 2 * SIDE]
        q_ref, v_ref, t_ref, st_ref, new_ref, nst_ref, bf_ref = refs[2 * SIDE :]
        for h, ins in ((0, a_in), (1, b_in)):
            line = place_ref[1 - h]
            turn = place_ref[h]
            row = jnp.broadcast_to(q_ref[pl.ds(line + h * SIDE, 1), :], (8, rows))
            row = pltpu.roll(row, ((SIDE - turn) % SIDE) * half, 1)
            weight = row.T[:half, 0:1]
            push = ins[0][...].astype(F32)
            for part in ins[1:]:
                push = push + part[...].astype(F32)
            g = weight * v_ref[h] - push
            cut = slice(h * half, (h + 1) * half)
            st = st_ref[cut, :] + jnp.sum(g * g, axis=1, keepdims=True) * (1.0 / width)
            nst_ref[cut, :] = st
            new = t_ref[cut, :] - LEARN * g / jnp.sqrt(st)
            new_ref[cut, :] = new
            bf_ref[cut, :] = new.astype(BF)

    full = lambda shape: pl.BlockSpec(shape, lambda i, s: (0,) * len(shape))
    return pl.pallas_call(
        body,
        name="source_update",
        out_shape=[
            jax.ShapeDtypeStruct((count, width), F32),
            jax.ShapeDtypeStruct((count, 1), F32),
            jax.ShapeDtypeStruct((count, width), BF),
        ],
        grid_spec=pltpu.PrefetchScalarGridSpec(
            num_scalar_prefetch=1,
            grid=(1,),
            in_specs=[full((half, width))] * (2 * SIDE)
            + [full((8, rows)), full((2, half, width)), full((count, width)), full((count, 1))],
            out_specs=[full((count, width)), full((count, 1)), full((count, width))],
        ),
        compiler_params=PARAMS,
    )(place, *parts_a, *parts_b, q_all, mix, table, state)


def slot_holding(sched_row, wanted):
    slots = jnp.arange(sched_row.shape[0], dtype=jnp.int32)
    return jnp.sum(slots * (sched_row[None, :] == wanted[:, None]).astype(jnp.int32), axis=1)


def shards(
    src_table,
    src_state,
    tgt_table,
    tgt_state,
    pair_source,
    pair_owner,
    pair_offset,
    negatives,
    plan,
):
    my_dom = lax.axis_index("dom")
    my_grp = lax.axis_index("grp")
    my_x, my_y = my_grp // SIDE, my_grp % SIDE
    src_count = src_table.shape[0]
    tgt_count = tgt_table.shape[0]
    rounds, doms = plan.shape
    base = my_grp * tgt_count
    place = jnp.stack([my_x, my_y, base]).astype(jnp.int32)
    base = base.reshape(1).astype(jnp.int32)

    count = negatives.shape[1]
    block = -(-count // (16 * SIDE * SIDE * 2)) * 16 * 2
    padded = jnp.pad(negatives[0], (0, block * SIDE * SIDE - count), constant_values=-1)
    grid = padded.reshape(SIDE, SIDE, 2, block // 2)
    grid = jnp.roll(jnp.roll(grid, -my_x, axis=0), -my_y, axis=1)
    ids = jnp.concatenate(
        [grid[:, :, 0].transpose(1, 0, 2).reshape(-1), grid[:, :, 1].reshape(-1)]
    )
    id_row, id_col = ids[None, :], ids[:, None]

    word = pair_source + ((pair_offset + pair_owner[:, :, 0] * tgt_count) << 7)
    line = jnp.stack(line_gather(word, 0))
    meta = jnp.concatenate(line_gather(line, 1))
    counts = [
        pair_counts(meta[:, r : r + 1, :], base, src_count, tgt_count) for r in range(rounds)
    ]

    here = jnp.arange(doms, dtype=jnp.int32)
    holder = here
    src_bf = src_table.astype(BF)
    src_state = src_state[:, None]
    tgt_state = tgt_state[:, None]
    for r in range(rounds):
        want = slot_holding(holder, plan[r])
        (src_bf,) = dom_fetch([src_bf], want, my_dom)
        src_table, src_state = dom_fetch([src_table, src_state], want, my_dom)
        holder = plan[r]
        masked = masked_negatives(tgt_table, id_col, base)
        part_a, part_b = group_scatter(masked, add_exact)
        neg_own = jnp.concatenate([add_exact(part_a), add_exact(part_b)], axis=0)
        neg_pieces = group_gather(neg_own)
        src_pieces = group_gather(src_bf)
        push, (grad, soft, q_part, mix, src_all) = score_round(
            place, src_pieces, neg_pieces, tgt_table, id_row, *counts[r]
        )
        q_all = group_sum(q_part)
        part_a, part_b = group_scatter(push, add_rounded)
        src_table, src_state, src_bf = source_update(
            place, part_a, part_b, q_all, mix, src_table, src_state
        )
        tgt_table, tgt_state = target_update(
            place, grad, soft, q_all, src_all, id_row, tgt_table, tgt_state
        )
    want = slot_holding(holder, here)
    src_table, src_state = dom_fetch([src_table, src_state], want, my_dom)
    return (src_table, src_state[:, 0], tgt_table, tgt_state[:, 0])


def solution(mesh):
    both = ("dom", "grp")
    return jax.shard_map(
        shards,
        mesh=mesh,
        in_specs=(
            P(both, None),
            P(both),
            P(both, None),
            P(both),
            P(None, both),
            P(None, both, None),
            P(None, both),
            P("dom", None),
            P(),
        ),
        out_specs=(P(both, None), P(both), P(both, None), P(both)),
        check_vma=False,
    )
```

```python
import jax
import jax.numpy as jnp
from jax import lax
from jax.experimental import pallas as pl
from jax.experimental.pallas import tpu as pltpu
from jax.sharding import PartitionSpec as P

LEARN = 0.1
BF = jnp.bfloat16
F32 = jnp.float32
I32 = jnp.int32
BIG = 3.0e38
TILE = 16


def swap_blocks(value):
    return lax.all_to_all(value, "grp", split_axis=0, concat_axis=0, tiled=True)


def spread(value):
    groups = lax.axis_size("grp")
    return swap_blocks(jnp.broadcast_to(value[None], (groups,) + value.shape))


def dom_fetch(value, want, my_dom):
    doms = want.shape[0]
    zs = doms // 2
    my_z, my_c = my_dom // 2, my_dom % 2
    other = lax.ppermute(value, "dom", [(i, i ^ 1) for i in range(doms)])

    def choose(dest):
        return jnp.where((want[dest] % 2) == my_c, value, other)

    from_k = (my_z - want[my_dom] // 2) % zs
    out = choose(my_dom)
    for k in range(1, zs):
        table = [(i, ((i // 2 + k) % zs) * 2 + i % 2) for i in range(doms)]
        got = lax.ppermute(choose(((my_z + k) % zs) * 2 + my_c), "dom", table)
        out = jnp.where(from_k == k, got, out)
    return out


def nn(a, b):
    return jnp.dot(a, b, preferred_element_type=F32)


def nt(a, b):
    return lax.dot_general(a, b, (((1,), (1,)), ((), ())), preferred_element_type=F32)


def one(mask):
    return mask.astype(F32).astype(BF)


def rows_iota(rows, cols):
    return lax.broadcasted_iota(I32, (rows, cols), 0)


def call(body, name, grid, prefetch, in_specs, out_specs, out_shape, scratch=(), limit=56):
    return pl.pallas_call(
        body,
        name=name,
        out_shape=out_shape,
        grid_spec=pltpu.PrefetchScalarGridSpec(
            num_scalar_prefetch=prefetch,
            grid=grid,
            in_specs=in_specs,
            out_specs=out_specs,
            scratch_shapes=list(scratch),
        ),
        compiler_params=pltpu.CompilerParams(vmem_limit_bytes=limit << 20),
    )


def full(shape):
    return pl.BlockSpec(shape, lambda *a: (0,) * len(shape))


def prepare(base, source, owner, offset, negs, groups, targets):
    rounds, pairs = source.shape
    slots = pairs // 4

    def body(base_ref, src_ref, own_ref, off_ref, neg_ref, word_ref, times_ref):
        before = one(rows_iota(pairs, pairs) < lax.broadcasted_iota(I32, (pairs, pairs), 1))
        for r in range(rounds):
            src, own, off = (ref[r : r + 1, :] for ref in (src_ref, own_ref, off_ref))
            hot = (own == rows_iota(groups, pairs)).astype(F32)
            rank = jnp.sum(nn(hot.astype(BF), before) * hot, axis=0, keepdims=True)
            slot = one(rank.astype(I32) == rows_iota(slots, pairs))
            parts = [(2 * src + 1), (off >> 5), (off & 31)]
            parts = jnp.concatenate([hot * part.astype(F32) for part in parts], axis=0)
            got = nt(parts.astype(BF), slot)
            a, b, c = (got[k * groups : (k + 1) * groups] for k in range(3))
            word_ref[:, r, :] = (a + 256.0 * (32.0 * b + c)).astype(I32)
        step = 128
        for k in range(targets // step):
            mine = rows_iota(step, neg_ref.shape[1]) + (base_ref[0] + k * step)
            count = jnp.sum((neg_ref[...] == mine).astype(F32), axis=1, keepdims=True)
            times_ref[k * step : (k + 1) * step, :] = jnp.broadcast_to(count, (step, 128))

    return call(
        body,
        "prepare",
        (1,),
        1,
        [full(source.shape)] * 3 + [full(negs.shape)],
        [full((groups, rounds, slots)), full((targets, 128))],
        [
            jax.ShapeDtypeStruct((groups, rounds, slots), I32),
            jax.ShapeDtypeStruct((targets, 128), F32),
        ],
    )(base, source, owner, offset, negs)


def pair_of(ref):
    return jnp.concatenate([ref[0], ref[1]], axis=1)


def wide(tile):
    return jnp.concatenate([tile, tile], axis=1)


def negative_stats(src_all, table_t, times):
    groups, width, count = src_all.shape
    targets = table_t.shape[1]
    cols = 2 * count
    steps = groups // 2
    big = 64

    def body(s_ref, t_ref, w_ref, out_ref, nat_ref, scores):
        @pl.when(pl.program_id(0) == 0)
        def _():
            nat_ref[...] = t_ref[...].T.astype(BF)

        scores[...] = nn(nat_ref[...], pair_of(s_ref))

        def largest(i, top):
            at = pl.ds(pl.multiple_of(i * big, big), big)
            tile = jnp.where(wide(w_ref[at, :]) > 0, scores[at, :], -BIG)
            return jnp.maximum(top, jnp.max(tile.reshape(big // 8, 8, cols), axis=0))

        top = lax.fori_loop(0, targets // big, largest, jnp.full((8, cols), -BIG, F32), unroll=2)
        top = jnp.max(top, axis=0, keepdims=True)

        def summed(i, acc):
            at = pl.ds(pl.multiple_of(i * big, big), big)
            w = wide(w_ref[at, :])
            tile = jnp.where(w > 0, w * jnp.exp(scores[at, :] - top), 0.0)
            return acc + jnp.sum(tile.reshape(big // 8, 8, cols), axis=0)

        acc = lax.fori_loop(0, targets // big, summed, jnp.zeros((8, cols), F32), unroll=2)
        out_ref[0:1, :] = top
        out_ref[1:2, :] = jnp.sum(acc, axis=0, keepdims=True)

    return call(
        body,
        "negative_stats",
        (steps,),
        0,
        [
            pl.BlockSpec((2, width, count), lambda p: (p, 0, 0)),
            full((width, targets)),
            full((targets, 128)),
        ],
        [pl.BlockSpec((2, cols), lambda p: (0, p)), full((targets, width))],
        [
            jax.ShapeDtypeStruct((2, groups * count), F32),
            jax.ShapeDtypeStruct((targets, width), BF),
        ],
        [pltpu.VMEM((targets, cols), F32)],
    )(src_all, table_t, times)


def pair_push(src_all, table, stats, words):
    groups, width, count = src_all.shape
    targets = table.shape[0]
    cols = 2 * count
    steps = groups // 2
    slots = words.shape[2]

    def body(s_ref, t_ref, st_ref, word_ref, nq_ref, soft_ref, q_ref, scores, number, mz):
        p = pl.program_id(0)

        @pl.when(p == 0)
        def _():
            tops = st_ref[:, 0, :]
            top = jnp.max(tops, axis=0, keepdims=True)
            mz[0:1, :] = top
            mz[1:2, :] = jnp.sum(st_ref[:, 1, :] * jnp.exp(tops - top), axis=0, keepdims=True)

        word = word_ref[0]
        half = lax.broadcasted_iota(I32, (1, slots), 1) // (slots // 2)
        src = jnp.where(word > 0, ((word & 255) >> 1) + half * count, -1)
        a = one(src == rows_iota(cols, slots))
        b = one((word >> 8) == rows_iota(targets, slots))
        number[...] = nt(b, a)
        scores[...] = nn(t_ref[...], pair_of(s_ref))
        lanes = pl.ds(pl.multiple_of(p * cols, cols), cols)
        top = jnp.broadcast_to(mz[0:1, lanes], (TILE, cols))
        total = jnp.broadcast_to(mz[1:2, lanes], (TILE, cols))
        inverse = 1.0 / total

        def tile(i, acc):
            at = pl.ds(pl.multiple_of(i * TILE, TILE), TILE)
            d = scores[at, :] - top
            x = jnp.exp(-jnp.abs(d))
            above = d > 0
            e1 = jnp.where(above, 1.0, x)
            e2 = total * jnp.where(above, x, 1.0)
            nq = number[at, :] * (e2 / (e1 + e2))
            nq_ref[0, at, :] = nq.astype(BF)
            soft_ref[0, at, :] = (e1 * inverse).astype(BF)
            return acc + nq

        acc = lax.fori_loop(
            0, targets // TILE, tile, jnp.zeros((TILE, cols), F32), unroll=4
        )
        q_ref[...] = jnp.sum(acc, axis=0, keepdims=True)

    block = pl.BlockSpec((1, targets, cols), lambda p: (p, 0, 0))
    return call(
        body,
        "pair_push",
        (steps,),
        0,
        [
            pl.BlockSpec((2, width, count), lambda p: (p, 0, 0)),
            full((targets, width)),
            full(stats.shape),
            pl.BlockSpec((1, 1, slots), lambda p: (p, 0, 0)),
        ],
        [block, block, pl.BlockSpec((1, cols), lambda p: (0, p))],
        [
            jax.ShapeDtypeStruct((steps, targets, cols), BF),
            jax.ShapeDtypeStruct((steps, targets, cols), BF),
            jax.ShapeDtypeStruct((1, groups * count), F32),
        ],
        [
            pltpu.VMEM((targets, cols), F32),
            pltpu.VMEM((targets, cols), F32),
            pltpu.VMEM((2, groups * count), F32),
        ],
    )(src_all, table, stats, words)


def source_push(nq, soft, q_all, times, table_t):
    steps, targets, cols = nq.shape
    width = table_t.shape[0]
    groups = q_all.shape[0]

    def body(nq_ref, soft_ref, q_ref, w_ref, t_ref, d_ref, u_ref, t_bf, q_sum):
        p = pl.program_id(0)

        @pl.when(p == 0)
        def _():
            t_bf[...] = t_ref[...].astype(BF)
            q_sum[...] = jnp.sum(q_ref[:, 0, :], axis=0, keepdims=True)

        lanes = pl.ds(pl.multiple_of(p * cols, cols), cols)
        q = jnp.broadcast_to(q_sum[0:1, lanes], (TILE, cols))

        def tile(i, carry):
            at = pl.ds(pl.multiple_of(i * TILE, TILE), TILE)
            push = wide(w_ref[at, :]) * (soft_ref[0, at, :].astype(F32) * q)
            d_ref[0, at, :] = (push - nq_ref[0, at, :].astype(F32)).astype(BF)
            return carry

        lax.fori_loop(0, targets // TILE, tile, 0, unroll=4)
        u = nn(t_bf[...], d_ref[0]).astype(BF)
        u_ref[0] = u[:, : cols // 2]
        u_ref[1] = u[:, cols // 2 :]

    block = pl.BlockSpec((1, targets, cols), lambda p: (p, 0, 0))
    return call(
        body,
        "source_push",
        (steps,),
        0,
        [block, block, full(q_all.shape), full((targets, 128)), full((width, targets))],
        [block, pl.BlockSpec((2, width, cols // 2), lambda p: (p, 0, 0))],
        [
            jax.ShapeDtypeStruct((steps, targets, cols), BF),
            jax.ShapeDtypeStruct((groups, width, cols // 2), BF),
        ],
        [pltpu.VMEM((width, targets), BF), pltpu.VMEM((1, steps * cols), F32)],
    )(nq, soft, q_all, times, table_t)


def target_update(push, src_all, table_t, state):
    steps, targets, cols = push.shape
    width = table_t.shape[0]
    count = src_all.shape[2]

    def body(d_ref, s_ref, t_ref, st_ref, new_ref, nst_ref, acc):
        p = pl.program_id(0)

        @pl.when(p == 0)
        def _():
            acc[...] = jnp.zeros_like(acc)

        acc[...] += nt(pair_of(s_ref), d_ref[0])

        @pl.when(p == steps - 1)
        def _():
            g = acc[...]
            st = st_ref[...] + jnp.sum(g * g, axis=0, keepdims=True) * (1.0 / width)
            nst_ref[...] = st
            new_ref[...] = t_ref[...] - LEARN * g / jnp.sqrt(st)

    return call(
        body,
        "target_update",
        (steps,),
        0,
        [
            pl.BlockSpec((1, targets, cols), lambda p: (p, 0, 0)),
            pl.BlockSpec((2, width, count), lambda p: (p, 0, 0)),
            full((width, targets)),
            full((1, targets)),
        ],
        [full((width, targets)), full((1, targets))],
        [
            jax.ShapeDtypeStruct((width, targets), F32),
            jax.ShapeDtypeStruct((1, targets), F32),
        ],
        [pltpu.VMEM((width, targets), F32)],
    )(push, src_all, table_t, state)


def source_update(parts, pack):
    groups, width, count = parts.shape

    def body(u_ref, pack_ref, new_ref):
        g = u_ref[0].astype(F32)
        for k in range(1, groups):
            g = g + u_ref[k].astype(F32)
        st = pack_ref[width : width + 1, :] + jnp.sum(g * g, axis=0, keepdims=True) * (1.0 / width)
        new_ref[:width, :] = pack_ref[:width, :] - LEARN * g / jnp.sqrt(st)
        new_ref[width:, :] = jnp.broadcast_to(st, (8, count))

    return call(
        body,
        "source_update",
        (1,),
        0,
        [full(parts.shape), full(pack.shape)],
        full(pack.shape),
        jax.ShapeDtypeStruct(pack.shape, F32),
    )(parts, pack)


def slot_holding(sched_row, wanted):
    slots = jnp.arange(sched_row.shape[0], dtype=I32)
    return jnp.sum(slots * (sched_row[None, :] == wanted[:, None]).astype(I32), axis=1)


def shards(
    src_table,
    src_state,
    tgt_table,
    tgt_state,
    pair_source,
    pair_owner,
    pair_offset,
    negatives,
    plan,
):
    my_dom = lax.axis_index("dom")
    groups = lax.axis_size("grp")
    count, width = src_table.shape
    targets = tgt_table.shape[0]
    rounds, doms = plan.shape
    base = (lax.axis_index("grp") * targets).astype(I32).reshape(1)

    lanes = -(-negatives.shape[1] // 128) * 128
    negs = jnp.pad(negatives, ((0, 0), (0, lanes - negatives.shape[1])), constant_values=-1)
    words, times = prepare(
        base, pair_source, pair_owner[:, :, 0], pair_offset, negs, groups, targets
    )
    words = swap_blocks(words)

    here = jnp.arange(doms, dtype=I32)
    holder = here
    pack = jnp.concatenate(
        [src_table.T, jnp.broadcast_to(src_state[None, :], (8, count))], axis=0
    )
    table_t = tgt_table.T
    state = tgt_state[None, :]
    for r in range(rounds):
        pack = dom_fetch(pack, slot_holding(holder, plan[r]), my_dom)
        holder = plan[r]
        src_all = spread(pack[:width].astype(BF))
        stats, table = negative_stats(src_all, table_t, times)
        stats = spread(stats)
        pairs = words[:, r, :].reshape(groups // 2, 1, -1)
        nq, soft, q = pair_push(src_all, table, stats, pairs)
        q_all = spread(q)
        push, parts = source_push(nq, soft, q_all, times, table_t)
        parts = swap_blocks(parts)
        pack = source_update(parts, pack)
        table_t, state = target_update(push, src_all, table_t, state)
    pack = dom_fetch(pack, slot_holding(holder, here), my_dom)
    return (pack[:width].T, pack[width], table_t.T, state[0])


def solution(mesh):
    both = ("dom", "grp")
    return jax.shard_map(
        shards,
        mesh=mesh,
        in_specs=(
            P(both, None),
            P(both),
            P(both, None),
            P(both),
            P(None, both),
            P(None, both, None),
            P(None, both),
            P("dom", None),
            P(),
        ),
        out_specs=(P(both, None), P(both), P(both, None), P(both)),
        check_vma=False,
    )
```

```python
import jax
import jax.numpy as jnp
from jax import lax
from jax.experimental import pallas as pl
from jax.experimental.pallas import tpu as pltpu
from jax.sharding import PartitionSpec as P

LEARN = 0.1
BF = jnp.bfloat16
F32 = jnp.float32
I32 = jnp.int32
BIG = 3.0e38
TILE = 16


def swap_blocks(value):
    return lax.all_to_all(value, "grp", split_axis=0, concat_axis=0, tiled=True)


def spread(value):
    groups = lax.axis_size("grp")
    return swap_blocks(jnp.broadcast_to(value[None], (groups,) + value.shape))


def group_sum(value):
    side = 4
    for axis in (0, 1):
        parts = [value]
        for k in range(1, side):
            dx, dy = (k, 0) if axis == 0 else (0, k)
            table = [
                (((i // side + dx) % side) * side + (i % side + dy) % side, i)
                for i in range(side * side)
            ]
            parts.append(lax.ppermute(value, "grp", table))
        value = (parts[0] + parts[1]) + (parts[2] + parts[3])
    return value


def dom_fetch(value, want, my_dom):
    doms = want.shape[0]
    zs = doms // 2
    my_z, my_c = my_dom // 2, my_dom % 2
    other = lax.ppermute(value, "dom", [(i, i ^ 1) for i in range(doms)])

    def choose(dest):
        return jnp.where((want[dest] % 2) == my_c, value, other)

    from_k = (my_z - want[my_dom] // 2) % zs
    out = choose(my_dom)
    for k in range(1, zs):
        table = [(i, ((i // 2 + k) % zs) * 2 + i % 2) for i in range(doms)]
        got = lax.ppermute(choose(((my_z + k) % zs) * 2 + my_c), "dom", table)
        out = jnp.where(from_k == k, got, out)
    return out


def nn(a, b):
    return jnp.dot(a, b, preferred_element_type=F32)


def nt(a, b):
    return lax.dot_general(a, b, (((1,), (1,)), ((), ())), preferred_element_type=F32)


def one(mask):
    return mask.astype(F32).astype(BF)


def rows_iota(rows, cols):
    return lax.broadcasted_iota(I32, (rows, cols), 0)


def call(body, name, grid, prefetch, in_specs, out_specs, out_shape, scratch=(), limit=56):
    return pl.pallas_call(
        body,
        name=name,
        out_shape=out_shape,
        grid_spec=pltpu.PrefetchScalarGridSpec(
            num_scalar_prefetch=prefetch,
            grid=grid,
            in_specs=in_specs,
            out_specs=out_specs,
            scratch_shapes=list(scratch),
        ),
        compiler_params=pltpu.CompilerParams(vmem_limit_bytes=limit << 20),
    )


def full(shape):
    return pl.BlockSpec(shape, lambda *a: (0,) * len(shape))


def prepare(base, source, owner, offset, negs, groups, targets):
    rounds, pairs = source.shape
    slots = pairs // 4

    def body(base_ref, src_ref, own_ref, off_ref, neg_ref, word_ref, times_ref):
        before = one(rows_iota(pairs, pairs) < lax.broadcasted_iota(I32, (pairs, pairs), 1))
        for r in range(rounds):
            src, own, off = (ref[r : r + 1, :] for ref in (src_ref, own_ref, off_ref))
            hot = (own == rows_iota(groups, pairs)).astype(F32)
            rank = jnp.sum(nn(hot.astype(BF), before) * hot, axis=0, keepdims=True)
            slot = one(rank.astype(I32) == rows_iota(slots, pairs))
            parts = [(2 * src + 1), (off >> 5), (off & 31)]
            parts = jnp.concatenate([hot * part.astype(F32) for part in parts], axis=0)
            got = nt(parts.astype(BF), slot)
            for k in range(3):
                part = got[k * groups : (k + 1) * groups].astype(BF)
                for j in range(slots // 128):
                    word_ref[r, k, j] = part[:, j * 128 : (j + 1) * 128]
        step = 128
        for k in range(targets // step):
            mine = rows_iota(step, neg_ref.shape[1]) + (base_ref[0] + k * step)
            count = jnp.sum((neg_ref[...] == mine).astype(F32), axis=1, keepdims=True)
            times_ref[k * step : (k + 1) * step, :] = jnp.broadcast_to(count, (step, 128))

    return call(
        body,
        "prepare",
        (1,),
        1,
        [full(source.shape)] * 3 + [full(negs.shape)],
        [full((rounds, 3, slots // 128, groups, 128)), full((targets, 128))],
        [
            jax.ShapeDtypeStruct((rounds, 3, slots // 128, groups, 128), BF),
            jax.ShapeDtypeStruct((targets, 128), F32),
        ],
    )(base, source, owner, offset, negs)


def named_rows(base, table_t, negs, groups):
    width, targets = table_t.shape
    lanes = negs.shape[1]
    half = width // 2

    def body(base_ref, t_ref, neg_ref, out_ref, nat_ref, bf_ref):
        t = t_ref[...]
        t_bf = t.astype(BF)
        bf_ref[...] = t_bf
        for k in range(lanes // 256):
            ids = neg_ref[:, k * 256 : (k + 1) * 256] - base_ref[0]
            rows = nn(t_bf, one(ids == rows_iota(targets, 256)))
            for j in range(2):
                for h in range(2):
                    piece = rows[h * half : (h + 1) * half, j * 128 : (j + 1) * 128]
                    out_ref[4 * k + 2 * j + h] = piece.astype(BF)
        nat_ref[...] = t.T.astype(BF)

    return call(
        body,
        "named_rows",
        (1,),
        1,
        [full((width, targets)), full(negs.shape)],
        [full((groups, half, 128)), full((targets, width)), full((width, targets))],
        [
            jax.ShapeDtypeStruct((groups, half, 128), BF),
            jax.ShapeDtypeStruct((targets, width), BF),
            jax.ShapeDtypeStruct((width, targets), BF),
        ],
    )(base, table_t, negs)


def merge_parts(parts, half):
    groups, _, lanes = parts.shape

    def body(in_ref, out_ref):
        total = in_ref[0].astype(F32)
        for k in range(1, groups):
            total = total + in_ref[k].astype(F32)
        out_ref[...] = total.astype(BF)

    return call(
        body,
        "merge_parts",
        (1,),
        0,
        [pl.BlockSpec((groups, half, lanes), lambda i: (0, 0, 0))],
        full((half, lanes)),
        jax.ShapeDtypeStruct((half, lanes), BF),
    )(parts)


def assemble(blocks, width):
    groups, depth, lanes = blocks.shape
    half, negs = width // 2, groups * lanes // 2

    def body(in_ref, nat_ref, t_ref, whole):
        for k in range(groups):
            at = slice((k // 2) * lanes, (k // 2 + 1) * lanes)
            whole[(k % 2) * half : (k % 2 + 1) * half, at] = in_ref[k].astype(F32)
        t_ref[...] = whole[...].astype(BF)
        nat_ref[...] = whole[...].T.astype(BF)

    return call(
        body,
        "assemble",
        (1,),
        0,
        [pl.BlockSpec((groups, half, lanes), lambda i: (0, width // half, 0))],
        [full((negs, width)), full((width, negs))],
        [jax.ShapeDtypeStruct((negs, width), BF), jax.ShapeDtypeStruct((width, negs), BF)],
        [pltpu.VMEM((width, negs), F32)],
    )(blocks)


def pair_of(ref):
    return jnp.concatenate([ref[0], ref[1]], axis=1)


def wide(tile):
    return jnp.concatenate([tile, tile], axis=1)


def softmax_stats(scores, named):
    rows, cols = scores.shape
    big = 64
    full_tiles = named // big

    def load(i):
        return scores[pl.ds(pl.multiple_of(i * big, big), big), :]

    def last():
        tile = scores[full_tiles * big : (full_tiles + 1) * big, :]
        return jnp.where(rows_iota(big, cols) < named - full_tiles * big, tile, -BIG)

    def fold(tile):
        return tile.reshape(big // 8, 8, cols)

    def largest(i, top):
        return jnp.maximum(top, jnp.max(fold(load(i)), axis=0))

    ragged = named % big != 0
    top = jnp.max(fold(last()), axis=0) if ragged else jnp.full((8, cols), -BIG, F32)
    top = lax.fori_loop(0, full_tiles, largest, top, unroll=3)
    top = jnp.max(top, axis=0, keepdims=True)

    def summed(i, acc):
        return acc + jnp.sum(fold(jnp.exp(load(i) - top)), axis=0)

    acc = jnp.sum(fold(jnp.exp(last() - top)), axis=0) if ragged else jnp.zeros((8, cols), F32)
    acc = lax.fori_loop(0, full_tiles, summed, acc, unroll=3)
    return top, jnp.sum(acc, axis=0, keepdims=True)


def pair_push(src_all, width, table, table_bf, neg, words, named):
    groups, _, count = src_all.shape
    targets = table.shape[0]
    negs = neg.shape[0]
    cols = 2 * count
    steps = groups // 2
    slots = words.shape[2]

    def body(s_ref, t_ref, tt_ref, neg_ref, word_ref, nq_ref, soft_ref, q_ref, u_ref, scores, number):
        s = pair_of(s_ref)
        scores[...] = nn(neg_ref[...], s)
        word = word_ref[0]
        half = lax.broadcasted_iota(I32, (1, slots), 1) // (slots // 2)
        src = jnp.where(word > 0, ((word & 255) >> 1) + half * count, -1)
        a = one(src == rows_iota(cols, slots))
        b = one((word >> 8) == rows_iota(targets, slots))
        number[...] = nt(b, a)
        top, total = softmax_stats(scores, named)
        scores[...] = nn(t_ref[...], s)
        top = jnp.broadcast_to(top, (TILE, cols))
        total = jnp.broadcast_to(total, (TILE, cols))
        inverse = 1.0 / total

        def tile(i, acc):
            at = pl.ds(pl.multiple_of(i * TILE, TILE), TILE)
            d = scores[at, :] - top
            x = jnp.exp(-jnp.abs(d))
            above = d > 0
            e1 = jnp.where(above, 1.0, x)
            e2 = total * jnp.where(above, x, 1.0)
            nq = number[at, :] * (e2 / (e1 + e2))
            nq_ref[0, at, :] = nq.astype(BF)
            soft_ref[0, at, :] = (e1 * inverse).astype(BF)
            return acc + nq

        acc = lax.fori_loop(
            0, targets // TILE, tile, jnp.zeros((TILE, cols), F32), unroll=4
        )
        q_ref[...] = jnp.sum(acc, axis=0, keepdims=True)
        u = nn(tt_ref[...], nq_ref[0]).astype(BF)
        u_ref[0] = u[:, :count]
        u_ref[1] = u[:, count:]

    block = pl.BlockSpec((1, targets, cols), lambda p: (p, 0, 0))
    pair = pl.BlockSpec((2, width, count), lambda p: (p, 0, 0))
    return call(
        body,
        "pair_push",
        (steps,),
        0,
        [
            pair,
            full((targets, width)),
            full((width, targets)),
            full((negs, width)),
            pl.BlockSpec((1, 1, slots), lambda p: (p, 0, 0)),
        ],
        [block, block, pl.BlockSpec((1, cols), lambda p: (0, p)), pair],
        [
            jax.ShapeDtypeStruct((steps, targets, cols), BF),
            jax.ShapeDtypeStruct((steps, targets, cols), BF),
            jax.ShapeDtypeStruct((1, groups * count), F32),
            jax.ShapeDtypeStruct((groups, width, count), BF),
        ],
        [pltpu.VMEM((max(targets, negs), cols), F32), pltpu.VMEM((targets, cols), F32)],
    )(src_all, table, table_bf, neg, words)


def own_mix(src, neg, neg_t, named):
    width, count = src.shape
    negs = neg.shape[0]

    def body(s_ref, neg_ref, negt_ref, out_ref, scores):
        scores[...] = nn(neg_ref[...], s_ref[...])
        top, total = softmax_stats(scores, named)
        weight = jnp.exp(scores[...] - top)
        weight = jnp.where(rows_iota(negs, count) < named, weight, 0.0).astype(BF)
        out_ref[...] = nn(negt_ref[...], weight) / total

    return call(
        body,
        "own_mix",
        (1,),
        0,
        [full((width, count)), full((negs, width)), full((width, negs))],
        full((width, count)),
        jax.ShapeDtypeStruct((width, count), F32),
        [pltpu.VMEM((negs, count), F32)],
    )(src, neg, neg_t)


def target_update(nq, soft, q_all, times, src_all, table_t, state):
    steps, targets, cols = nq.shape
    width = table_t.shape[0]
    count = src_all.shape[2]

    def body(nq_ref, soft_ref, q_ref, w_ref, s_ref, t_ref, st_ref, new_ref, nst_ref, acc, d_buf):
        p = pl.program_id(0)

        @pl.when(p == 0)
        def _():
            acc[...] = jnp.zeros_like(acc)

        lanes = pl.ds(pl.multiple_of(p * cols, cols), cols)
        q = jnp.broadcast_to(q_ref[0:1, lanes], (TILE, cols))

        def tile(i, carry):
            at = pl.ds(pl.multiple_of(i * TILE, TILE), TILE)
            push = wide(w_ref[at, :]) * (soft_ref[0, at, :].astype(F32) * q)
            d_buf[at, :] = (push - nq_ref[0, at, :].astype(F32)).astype(BF)
            return carry

        lax.fori_loop(0, targets // TILE, tile, 0, unroll=4)
        acc[...] += nt(pair_of(s_ref), d_buf[...])

        @pl.when(p == steps - 1)
        def _():
            g = acc[...]
            st = st_ref[...] + jnp.sum(g * g, axis=0, keepdims=True) * (1.0 / width)
            nst_ref[...] = st
            new_ref[...] = t_ref[...] - LEARN * g / jnp.sqrt(st)

    block = pl.BlockSpec((1, targets, cols), lambda p: (p, 0, 0))
    return call(
        body,
        "target_update",
        (steps,),
        0,
        [
            block,
            block,
            full(q_all.shape),
            full((targets, 128)),
            pl.BlockSpec((2, width, count), lambda p: (p, 0, 0)),
            full((width, targets)),
            full((1, targets)),
        ],
        [full((width, targets)), full((1, targets))],
        [
            jax.ShapeDtypeStruct((width, targets), F32),
            jax.ShapeDtypeStruct((1, targets), F32),
        ],
        [
            pltpu.VMEM((width, targets), F32),
            pltpu.VMEM((targets, cols), BF),
        ],
    )(nq, soft, q_all, times, src_all, table_t, state)


def source_update(me, parts, q_all, mix, pack):
    groups, width, count = parts.shape

    def body(me_ref, u_ref, q_ref, mix_ref, pack_ref, new_ref, bf_ref):
        at = pl.ds(pl.multiple_of(me_ref[0] * count, count), count)
        q = q_ref[0:1, at]
        push = u_ref[0].astype(F32)
        for k in range(1, groups):
            push = push + u_ref[k].astype(F32)
        g = q * mix_ref[...] - push
        st = pack_ref[width : width + 1, :] + jnp.sum(g * g, axis=0, keepdims=True) * (1.0 / width)
        new = pack_ref[:width, :] - LEARN * g / jnp.sqrt(st)
        new_ref[:width, :] = new
        new_ref[width:, :] = jnp.broadcast_to(st, (8, count))
        bf_ref[...] = new.astype(BF)

    return call(
        body,
        "source_update",
        (1,),
        1,
        [full(parts.shape), full(q_all.shape), full((width, count)), full(pack.shape)],
        [full(pack.shape), full((width, count))],
        [jax.ShapeDtypeStruct(pack.shape, F32), jax.ShapeDtypeStruct((width, count), BF)],
    )(me, parts, q_all, mix, pack)


def slot_holding(sched_row, wanted):
    slots = jnp.arange(sched_row.shape[0], dtype=I32)
    return jnp.sum(slots * (sched_row[None, :] == wanted[:, None]).astype(I32), axis=1)


def shards(
    src_table,
    src_state,
    tgt_table,
    tgt_state,
    pair_source,
    pair_owner,
    pair_offset,
    negatives,
    plan,
):
    my_dom = lax.axis_index("dom")
    groups = lax.axis_size("grp")
    count, width = src_table.shape
    targets = tgt_table.shape[0]
    rounds, doms = plan.shape
    me = lax.axis_index("grp").astype(I32).reshape(1)
    base = me * targets
    named = negatives.shape[1]

    half = width // 2
    lanes = groups // 2 * 128
    negs = jnp.pad(negatives, ((0, 0), (0, lanes - named)), constant_values=-1)
    words, times = prepare(
        base, pair_source, pair_owner[:, :, 0], pair_offset, negs, groups, targets
    )
    words = words.transpose(3, 0, 1, 2, 4).reshape(groups, -1, 128)
    pad = -words.shape[1] % 8
    words = jnp.pad(words, ((0, 0), (0, pad), (0, 0)))

    here = jnp.arange(doms, dtype=I32)
    src = src_table.T.astype(BF)
    pack = jnp.concatenate(
        [src_table.T, jnp.broadcast_to(src_state[None, :], (8, count))], axis=0
    )
    table_t = tgt_table.T
    state = tgt_state[None, :]
    for r in range(rounds):
        rows, table, table_bf = named_rows(base, table_t, negs, groups)
        if r == 0:
            rows = swap_blocks(jnp.concatenate([rows, words], axis=1))
            code = rows[:, half : half + rounds * 6].astype(I32).reshape(groups, rounds, 3, 256)
            src = dom_fetch(src, plan[0], my_dom)
            pack = dom_fetch(pack, plan[0], my_dom)
            holder = plan[0]
            pairs = code[:, :, 0] + 256 * (32 * code[:, :, 1] + code[:, :, 2])
        else:
            rows, parts = lax.optimization_barrier((rows, parts))
            rows = swap_blocks(rows)
            pack, src = source_update(me, parts, q_all, mix, pack)
            want = slot_holding(holder, plan[r])
            holder = plan[r]
            src = dom_fetch(src, want, my_dom)
            pack = dom_fetch(pack, want, my_dom)
        src_all = spread(jnp.concatenate([src, merge_parts(rows, half)], axis=0))
        neg, neg_t = assemble(src_all, width)
        nq, soft, q, parts = pair_push(
            src_all, width, table, table_bf, neg, pairs[:, r].reshape(groups // 2, 1, -1), named
        )
        parts = swap_blocks(parts)
        mix = own_mix(src, neg, neg_t, named)
        q_all = group_sum(q)
        table_t, state = target_update(nq, soft, q_all, times, src_all, table_t, state)
    pack, src = source_update(me, parts, q_all, mix, pack)
    pack = dom_fetch(pack, slot_holding(holder, here), my_dom)
    return (pack[:width].T, pack[width], table_t.T, state[0])


def solution(mesh):
    both = ("dom", "grp")
    return jax.shard_map(
        shards,
        mesh=mesh,
        in_specs=(
            P(both, None),
            P(both),
            P(both, None),
            P(both),
            P(None, both),
            P(None, both, None),
            P(None, both),
            P("dom", None),
            P(),
        ),
        out_specs=(P(both, None), P(both), P(both, None), P(both)),
        check_vma=False,
    )
```

```python
import jax
import jax.numpy as jnp
from jax import lax
from jax.experimental import pallas as pl
from jax.experimental.pallas import tpu as pltpu
from jax.sharding import PartitionSpec as P

LEARN = 0.1
BF = jnp.bfloat16
F32 = jnp.float32
I32 = jnp.int32
BIG = 3.0e38
TILE = 16


def swap_blocks(value):
    return lax.all_to_all(value, "grp", split_axis=0, concat_axis=0, tiled=True)


def spread(value):
    groups = lax.axis_size("grp")
    return swap_blocks(jnp.broadcast_to(value[None], (groups,) + value.shape))


def dom_fetch(value, want, my_dom):
    doms = want.shape[0]
    zs = doms // 2
    my_z, my_c = my_dom // 2, my_dom % 2
    other = lax.ppermute(value, "dom", [(i, i ^ 1) for i in range(doms)])

    def choose(dest):
        return jnp.where((want[dest] % 2) == my_c, value, other)

    from_k = (my_z - want[my_dom] // 2) % zs
    out = choose(my_dom)
    for k in range(1, zs):
        table = [(i, ((i // 2 + k) % zs) * 2 + i % 2) for i in range(doms)]
        got = lax.ppermute(choose(((my_z + k) % zs) * 2 + my_c), "dom", table)
        out = jnp.where(from_k == k, got, out)
    return out


def nn(a, b):
    return jnp.dot(a, b, preferred_element_type=F32)


def nt(a, b):
    return lax.dot_general(a, b, (((1,), (1,)), ((), ())), preferred_element_type=F32)


def one(mask):
    return mask.astype(F32).astype(BF)


def rows_iota(rows, cols):
    return lax.broadcasted_iota(I32, (rows, cols), 0)


def call(body, name, grid, prefetch, in_specs, out_specs, out_shape, scratch=(), limit=56):
    return pl.pallas_call(
        body,
        name=name,
        out_shape=out_shape,
        grid_spec=pltpu.PrefetchScalarGridSpec(
            num_scalar_prefetch=prefetch,
            grid=grid,
            in_specs=in_specs,
            out_specs=out_specs,
            scratch_shapes=list(scratch),
        ),
        compiler_params=pltpu.CompilerParams(vmem_limit_bytes=limit << 20),
    )


def full(shape):
    return pl.BlockSpec(shape, lambda *a: (0,) * len(shape))


def prepare(base, source, owner, offset, negs, groups, targets):
    rounds, pairs = source.shape
    slots = pairs // 4

    def body(base_ref, src_ref, own_ref, off_ref, neg_ref, word_ref, times_ref):
        before = one(rows_iota(pairs, pairs) < lax.broadcasted_iota(I32, (pairs, pairs), 1))
        for r in range(rounds):
            src, own, off = (ref[r : r + 1, :] for ref in (src_ref, own_ref, off_ref))
            hot = (own == rows_iota(groups, pairs)).astype(F32)
            rank = jnp.sum(nn(hot.astype(BF), before) * hot, axis=0, keepdims=True)
            slot = one(rank.astype(I32) == rows_iota(slots, pairs))
            parts = [(2 * src + 1), (off >> 5), (off & 31)]
            parts = jnp.concatenate([hot * part.astype(F32) for part in parts], axis=0)
            got = nt(parts.astype(BF), slot)
            a, b, c = (got[k * groups : (k + 1) * groups] for k in range(3))
            word_ref[:, r, :] = (a + 256.0 * (32.0 * b + c)).astype(I32)
        step = 128
        for k in range(targets // step):
            mine = rows_iota(step, neg_ref.shape[1]) + (base_ref[0] + k * step)
            count = jnp.sum((neg_ref[...] == mine).astype(F32), axis=1, keepdims=True)
            times_ref[k * step : (k + 1) * step, :] = jnp.broadcast_to(count, (step, 128))

    return call(
        body,
        "prepare",
        (1,),
        1,
        [full(source.shape)] * 3 + [full(negs.shape)],
        [full((groups, rounds, slots)), full((targets, 128))],
        [
            jax.ShapeDtypeStruct((groups, rounds, slots), I32),
            jax.ShapeDtypeStruct((targets, 128), F32),
        ],
    )(base, source, owner, offset, negs)


def pair_of(ref):
    return jnp.concatenate([ref[0], ref[1]], axis=1)


def wide(tile):
    return jnp.concatenate([tile, tile], axis=1)


def pair_counts(words, count, targets):
    steps, _, slots = words.shape
    cols = 2 * count

    def body(word_ref, out_ref):
        word = word_ref[0]
        half = lax.broadcasted_iota(I32, (1, slots), 1) // (slots // 2)
        src = jnp.where(word > 0, ((word & 255) >> 1) + half * count, -1)
        a = one(src == rows_iota(cols, slots))
        b = one((word >> 8) == rows_iota(targets, slots))
        out_ref[0] = nt(b, a).astype(BF)

    return call(
        body,
        "pair_counts",
        (steps,),
        0,
        [pl.BlockSpec((1, 1, slots), lambda p: (p, 0, 0))],
        pl.BlockSpec((1, targets, cols), lambda p: (p, 0, 0)),
        jax.ShapeDtypeStruct((steps, targets, cols), BF),
    )(words)


def both_ways(table_t):
    width, targets = table_t.shape

    def body(t_ref, nat_ref, bf_ref):
        nat_ref[...] = t_ref[...].T.astype(BF)
        bf_ref[...] = t_ref[...].astype(BF)

    return call(
        body,
        "both_ways",
        (1,),
        0,
        [full((width, targets))],
        [full((targets, width)), full((width, targets))],
        [
            jax.ShapeDtypeStruct((targets, width), BF),
            jax.ShapeDtypeStruct((width, targets), BF),
        ],
    )(table_t)


def negative_stats(src_all, table, table_bf, times):
    groups, width, count = src_all.shape
    targets = table.shape[0]
    cols = 2 * count
    steps = groups // 2
    big = 64

    def body(s_ref, t_ref, tt_ref, w_ref, out_ref, mix_ref, scores, weight):
        scores[...] = nn(t_ref[...], pair_of(s_ref))

        def largest(i, top):
            at = pl.ds(pl.multiple_of(i * big, big), big)
            tile = jnp.where(wide(w_ref[at, :]) > 0, scores[at, :], -BIG)
            return jnp.maximum(top, jnp.max(tile.reshape(big // 8, 8, cols), axis=0))

        top = lax.fori_loop(0, targets // big, largest, jnp.full((8, cols), -BIG, F32), unroll=4)
        top = jnp.max(top, axis=0, keepdims=True)

        def summed(i, acc):
            at = pl.ds(pl.multiple_of(i * big, big), big)
            w = wide(w_ref[at, :])
            tile = jnp.where(w > 0, w * jnp.exp(scores[at, :] - top), 0.0)
            weight[at, :] = tile.astype(BF)
            return acc + jnp.sum(tile.reshape(big // 8, 8, cols), axis=0)

        acc = lax.fori_loop(0, targets // big, summed, jnp.zeros((8, cols), F32), unroll=4)
        out_ref[0:1, :] = top
        out_ref[1:2, :] = jnp.sum(acc, axis=0, keepdims=True)
        mix = nn(tt_ref[...], weight[...]).astype(BF)
        mix_ref[0] = mix[:, :count]
        mix_ref[1] = mix[:, count:]

    pair = pl.BlockSpec((2, width, count), lambda p: (p, 0, 0))
    return call(
        body,
        "negative_stats",
        (steps,),
        0,
        [pair, full((targets, width)), full((width, targets)), full((targets, 128))],
        [pl.BlockSpec((2, cols), lambda p: (0, p)), pair],
        [
            jax.ShapeDtypeStruct((2, groups * count), F32),
            jax.ShapeDtypeStruct((groups, width, count), BF),
        ],
        [pltpu.VMEM((targets, cols), F32), pltpu.VMEM((targets, cols), BF)],
    )(src_all, table, table_bf, times)


def pair_push(src_all, table, table_bf, stats, counts):
    groups, width, count = src_all.shape
    targets = table.shape[0]
    cols = 2 * count
    steps = groups // 2
    tail = 16

    def body(s_ref, t_ref, tt_ref, st_ref, n_ref, nq_ref, soft_ref, u_ref, scores, mz):
        p = pl.program_id(0)

        @pl.when(p == 0)
        def _():
            tops = st_ref[:, 0, :]
            top = jnp.max(tops, axis=0, keepdims=True)
            mz[0:1, :] = top
            mz[1:2, :] = jnp.sum(st_ref[:, 1, :] * jnp.exp(tops - top), axis=0, keepdims=True)

        scores[...] = nn(t_ref[...], pair_of(s_ref))
        lanes = pl.ds(pl.multiple_of(p * cols, cols), cols)
        top = jnp.broadcast_to(mz[0:1, lanes], (TILE, cols))
        total = jnp.broadcast_to(mz[1:2, lanes], (TILE, cols))
        inverse = 1.0 / total

        def tile(i, acc):
            at = pl.ds(pl.multiple_of(i * TILE, TILE), TILE)
            d = scores[at, :] - top
            x = jnp.exp(-jnp.abs(d))
            above = d > 0
            e1 = jnp.where(above, 1.0, x)
            e2 = total * jnp.where(above, x, 1.0)
            nq = n_ref[0, at, :].astype(F32) * (e2 / (e1 + e2))
            nq_ref[0, at, :] = nq.astype(BF)
            soft_ref[0, at, :] = (e1 * inverse).astype(BF)
            return acc + nq

        acc = lax.fori_loop(
            0, targets // TILE, tile, jnp.zeros((TILE, cols), F32), unroll=8
        )
        q = jnp.sum(acc, axis=0, keepdims=True)
        high = q.astype(BF).astype(F32)
        row = rows_iota(tail, cols)
        ends = jnp.where(row == 0, high, jnp.where(row == 1, q - high, 0.0)).astype(BF)
        u = nn(tt_ref[...], nq_ref[0]).astype(BF)
        for k in range(2):
            u_ref[k, :width, :] = u[:, k * count : (k + 1) * count]
            u_ref[k, width:, :] = ends[:, k * count : (k + 1) * count]

    block = pl.BlockSpec((1, targets, cols), lambda p: (p, 0, 0))
    return call(
        body,
        "pair_push",
        (steps,),
        0,
        [
            pl.BlockSpec((2, width, count), lambda p: (p, 0, 0)),
            full((targets, width)),
            full((width, targets)),
            full(stats.shape),
            block,
        ],
        [block, block, pl.BlockSpec((2, width + tail, count), lambda p: (p, 0, 0))],
        [
            jax.ShapeDtypeStruct((steps, targets, cols), BF),
            jax.ShapeDtypeStruct((steps, targets, cols), BF),
            jax.ShapeDtypeStruct((groups, width + tail, count), BF),
        ],
        [pltpu.VMEM((targets, cols), F32), pltpu.VMEM((2, groups * count), F32)],
    )(src_all, table, table_bf, stats, counts)


def target_update(nq, soft, q_all, times, src_all, table_t, state):
    steps, targets, cols = nq.shape
    width = table_t.shape[0]
    count = src_all.shape[2]

    def body(
        nq_ref, soft_ref, q_ref, w_ref, s_ref, t_ref, st_ref, new_ref, nst_ref, nat_ref, bf_ref, acc, d_buf
    ):
        p = pl.program_id(0)

        @pl.when(p == 0)
        def _():
            acc[...] = jnp.zeros_like(acc)

        lanes = pl.ds(pl.multiple_of(p * cols, cols), cols)
        q = jnp.broadcast_to(q_ref[0:1, lanes], (TILE, cols))

        def tile(i, carry):
            at = pl.ds(pl.multiple_of(i * TILE, TILE), TILE)
            push = wide(w_ref[at, :]) * (soft_ref[0, at, :].astype(F32) * q)
            d_buf[at, :] = (push - nq_ref[0, at, :].astype(F32)).astype(BF)
            return carry

        lax.fori_loop(0, targets // TILE, tile, 0, unroll=8)
        acc[...] += nt(pair_of(s_ref), d_buf[...])

        @pl.when(p == steps - 1)
        def _():
            g = acc[...]
            st = st_ref[...] + jnp.sum(g * g, axis=0, keepdims=True) * (1.0 / width)
            nst_ref[...] = st
            new = t_ref[...] - LEARN * g / jnp.sqrt(st)
            new_ref[...] = new
            bf_ref[...] = new.astype(BF)
            nat_ref[...] = new.T.astype(BF)

    block = pl.BlockSpec((1, targets, cols), lambda p: (p, 0, 0))
    return call(
        body,
        "target_update",
        (steps,),
        0,
        [
            block,
            block,
            full(q_all.shape),
            full((targets, 128)),
            pl.BlockSpec((2, width, count), lambda p: (p, 0, 0)),
            full((width, targets)),
            full((1, targets)),
        ],
        [
            full((width, targets)),
            full((1, targets)),
            full((targets, width)),
            full((width, targets)),
        ],
        [
            jax.ShapeDtypeStruct((width, targets), F32),
            jax.ShapeDtypeStruct((1, targets), F32),
            jax.ShapeDtypeStruct((targets, width), BF),
            jax.ShapeDtypeStruct((width, targets), BF),
        ],
        [pltpu.VMEM((width, targets), F32), pltpu.VMEM((targets, cols), BF)],
    )(nq, soft, q_all, times, src_all, table_t, state)


def source_update(me, parts, mixes, stats, pack):
    groups, width, count = mixes.shape

    def body(me_ref, u_ref, v_ref, st_ref, pack_ref, new_ref, bf_ref, q_ref):
        at = pl.ds(pl.multiple_of(me_ref[0] * count, count), count)
        tops = st_ref[:, 0, at]
        top = jnp.max(tops, axis=0, keepdims=True)
        share = jnp.exp(tops - top)
        share = share / jnp.sum(st_ref[:, 1, at] * share, axis=0, keepdims=True)
        q = jnp.zeros((1, count), F32)
        push = jnp.zeros((width, count), F32)
        mix = jnp.zeros((width, count), F32)
        for k in range(groups):
            ends = u_ref[k, width:, :].astype(F32)
            q = q + ends[0:1] + ends[1:2]
            push = push + u_ref[k, :width, :].astype(F32)
            mix = mix + share[k : k + 1] * v_ref[k].astype(F32)
        g = q * mix - push
        st = pack_ref[width : width + 1, :] + jnp.sum(g * g, axis=0, keepdims=True) * (1.0 / width)
        new = pack_ref[:width, :] - LEARN * g / jnp.sqrt(st)
        new_ref[:width, :] = new
        new_ref[width:, :] = jnp.broadcast_to(st, (8, count))
        bf_ref[...] = new.astype(BF)
        q_ref[...] = q

    return call(
        body,
        "source_update",
        (1,),
        1,
        [full(parts.shape), full(mixes.shape), full(stats.shape), full(pack.shape)],
        [full(pack.shape), full((width, count)), full((1, count))],
        [
            jax.ShapeDtypeStruct(pack.shape, F32),
            jax.ShapeDtypeStruct((width, count), BF),
            jax.ShapeDtypeStruct((1, count), F32),
        ],
    )(me, parts, mixes, stats, pack)


def slot_holding(sched_row, wanted):
    slots = jnp.arange(sched_row.shape[0], dtype=I32)
    return jnp.sum(slots * (sched_row[None, :] == wanted[:, None]).astype(I32), axis=1)


def shards(
    src_table,
    src_state,
    tgt_table,
    tgt_state,
    pair_source,
    pair_owner,
    pair_offset,
    negatives,
    plan,
):
    my_dom = lax.axis_index("dom")
    groups = lax.axis_size("grp")
    count, width = src_table.shape
    targets = tgt_table.shape[0]
    rounds, doms = plan.shape
    me = lax.axis_index("grp").astype(I32).reshape(1)
    base = me * targets

    lanes = -(-negatives.shape[1] // 128) * 128
    negs = jnp.pad(negatives, ((0, 0), (0, lanes - negatives.shape[1])), constant_values=-1)
    words, times = prepare(
        base, pair_source, pair_owner[:, :, 0], pair_offset, negs, groups, targets
    )
    words = swap_blocks(words)
    words = words.transpose(1, 0, 2).reshape(rounds * groups // 2, 1, -1)

    here = jnp.arange(doms, dtype=I32)
    src = src_table.T.astype(BF)
    pack = jnp.concatenate(
        [src_table.T, jnp.broadcast_to(src_state[None, :], (8, count))], axis=0
    )
    table_t = tgt_table.T
    state = tgt_state[None, :]
    table, table_bf = both_ways(table_t)
    want = plan[0]
    for r in range(rounds):
        src = dom_fetch(src, want, my_dom)
        pack = dom_fetch(pack, want, my_dom)
        if r:
            src, q_all = lax.optimization_barrier((src, q_all))
            src_all = spread(src)
            table_t, state, table, table_bf = target_update(
                nq, soft, q_all, times, src_old, table_t, state
            )
        else:
            src, words = lax.optimization_barrier((src, words))
            counts = pair_counts(words, count, targets)
            counts = counts.reshape(rounds, groups // 2, targets, 2 * count)
            src_all = spread(src)
        stats, mixes = negative_stats(src_all, table, table_bf, times)
        stats = spread(stats)
        stats, mixes = lax.optimization_barrier((stats, mixes))
        mixes = swap_blocks(mixes)
        nq, soft, parts = pair_push(src_all, table, table_bf, stats, counts[r])
        parts = swap_blocks(parts)
        pack, src, q = source_update(me, parts, mixes, stats, pack)
        q_all = spread(q).reshape(1, groups * count)
        src_old = src_all
        goal = plan[r + 1] if r + 1 < rounds else here
        want = slot_holding(plan[r], goal)
    pack = dom_fetch(pack, want, my_dom)
    table_t, state, _, _ = target_update(nq, soft, q_all, times, src_old, table_t, state)
    return (pack[:width].T, pack[width], table_t.T, state[0])


def solution(mesh):
    both = ("dom", "grp")
    return jax.shard_map(
        shards,
        mesh=mesh,
        in_specs=(
            P(both, None),
            P(both),
            P(both, None),
            P(both),
            P(None, both),
            P(None, both, None),
            P(None, both),
            P("dom", None),
            P(),
        ),
        out_specs=(P(both, None), P(both), P(both, None), P(both)),
        check_vma=False,
    )
```

```python
import jax
import jax.numpy as jnp
from jax import lax
from jax.experimental import pallas as pl
from jax.experimental.pallas import tpu as pltpu
from jax.sharding import PartitionSpec as P

LEARN = 0.1
BF = jnp.bfloat16
F32 = jnp.float32
I32 = jnp.int32
BIG = 3.0e38
TILE = 16
UNROLL_A, UNROLL_B, UNROLL_C = 2, 4, 4


def swap_blocks(value):
    return lax.all_to_all(value, "grp", split_axis=0, concat_axis=0, tiled=True)


def spread(value):
    groups = lax.axis_size("grp")
    return swap_blocks(jnp.broadcast_to(value[None], (groups,) + value.shape))


def dom_fetch(value, want, my_dom):
    doms = want.shape[0]
    zs = doms // 2
    my_z, my_c = my_dom // 2, my_dom % 2
    other = lax.ppermute(value, "dom", [(i, i ^ 1) for i in range(doms)])

    def choose(dest):
        return jnp.where((want[dest] % 2) == my_c, value, other)

    from_k = (my_z - want[my_dom] // 2) % zs
    out = choose(my_dom)
    for k in range(1, zs):
        table = [(i, ((i // 2 + k) % zs) * 2 + i % 2) for i in range(doms)]
        got = lax.ppermute(choose(((my_z + k) % zs) * 2 + my_c), "dom", table)
        out = jnp.where(from_k == k, got, out)
    return out


def nn(a, b):
    return jnp.dot(a, b, preferred_element_type=F32)


def nt(a, b):
    return lax.dot_general(a, b, (((1,), (1,)), ((), ())), preferred_element_type=F32)


def one(mask):
    return mask.astype(F32).astype(BF)


def rows_iota(rows, cols):
    return lax.broadcasted_iota(I32, (rows, cols), 0)


def call(body, name, grid, prefetch, in_specs, out_specs, out_shape, scratch=(), limit=56):
    return pl.pallas_call(
        body,
        name=name,
        out_shape=out_shape,
        grid_spec=pltpu.PrefetchScalarGridSpec(
            num_scalar_prefetch=prefetch,
            grid=grid,
            in_specs=in_specs,
            out_specs=out_specs,
            scratch_shapes=list(scratch),
        ),
        compiler_params=pltpu.CompilerParams(vmem_limit_bytes=limit << 20),
    )


def full(shape):
    return pl.BlockSpec(shape, lambda *a: (0,) * len(shape))


def prepare(base, source, owner, offset, negs, groups, targets):
    rounds, pairs = source.shape
    slots = pairs // 4

    def body(base_ref, src_ref, own_ref, off_ref, neg_ref, word_ref, times_ref):
        before = one(rows_iota(pairs, pairs) < lax.broadcasted_iota(I32, (pairs, pairs), 1))
        for r in range(rounds):
            src, own, off = (ref[r : r + 1, :] for ref in (src_ref, own_ref, off_ref))
            hot = (own == rows_iota(groups, pairs)).astype(F32)
            rank = jnp.sum(nn(hot.astype(BF), before) * hot, axis=0, keepdims=True)
            slot = one(rank.astype(I32) == rows_iota(slots, pairs))
            parts = [(2 * src + 1), (off >> 5), (off & 31)]
            parts = jnp.concatenate([hot * part.astype(F32) for part in parts], axis=0)
            got = nt(parts.astype(BF), slot)
            a, b, c = (got[k * groups : (k + 1) * groups] for k in range(3))
            word_ref[:, r, :] = (a + 256.0 * (32.0 * b + c)).astype(I32)
        step = 128
        for k in range(targets // step):
            mine = rows_iota(step, neg_ref.shape[1]) + (base_ref[0] + k * step)
            count = jnp.sum((neg_ref[...] == mine).astype(F32), axis=1, keepdims=True)
            times_ref[k * step : (k + 1) * step, :] = jnp.broadcast_to(count, (step, 128))

    return call(
        body,
        "prepare",
        (1,),
        1,
        [full(source.shape)] * 3 + [full(negs.shape)],
        [full((groups, rounds, slots)), full((targets, 128))],
        [
            jax.ShapeDtypeStruct((groups, rounds, slots), I32),
            jax.ShapeDtypeStruct((targets, 128), F32),
        ],
    )(base, source, owner, offset, negs)


def pair_of(ref):
    return jnp.concatenate([ref[0], ref[1]], axis=1)


def wide(tile):
    return jnp.concatenate([tile, tile], axis=1)


def pair_counts(words, count, targets):
    steps, _, slots = words.shape
    cols = 2 * count

    def body(word_ref, out_ref):
        word = word_ref[0]
        half = lax.broadcasted_iota(I32, (1, slots), 1) // (slots // 2)
        src = jnp.where(word > 0, ((word & 255) >> 1) + half * count, -1)
        a = one(src == rows_iota(cols, slots))
        b = one((word >> 8) == rows_iota(targets, slots))
        out_ref[0] = nt(b, a).astype(BF)

    return call(
        body,
        "pair_counts",
        (steps,),
        0,
        [pl.BlockSpec((1, 1, slots), lambda p: (p, 0, 0))],
        pl.BlockSpec((1, targets, cols), lambda p: (p, 0, 0)),
        jax.ShapeDtypeStruct((steps, targets, cols), BF),
    )(words)


def both_ways(table_t):
    width, targets = table_t.shape

    def body(t_ref, nat_ref, bf_ref):
        nat_ref[...] = t_ref[...].T.astype(BF)
        bf_ref[...] = t_ref[...].astype(BF)

    return call(
        body,
        "both_ways",
        (1,),
        0,
        [full((width, targets))],
        [full((targets, width)), full((width, targets))],
        [
            jax.ShapeDtypeStruct((targets, width), BF),
            jax.ShapeDtypeStruct((width, targets), BF),
        ],
    )(table_t)


def negative_stats(src_all, table, times):
    groups, width, count = src_all.shape
    targets = table.shape[0]
    cols = 2 * count
    steps = groups // 2
    big = 64

    def body(s_ref, t_ref, w_ref, out_ref, scores):
        scores[...] = nn(t_ref[...], pair_of(s_ref))

        def largest(i, top):
            at = pl.ds(pl.multiple_of(i * big, big), big)
            tile = jnp.where(wide(w_ref[at, :]) > 0, scores[at, :], -BIG)
            return jnp.maximum(top, jnp.max(tile.reshape(big // 8, 8, cols), axis=0))

        top = lax.fori_loop(0, targets // big, largest, jnp.full((8, cols), -BIG, F32), unroll=UNROLL_A)
        top = jnp.max(top, axis=0, keepdims=True)

        def summed(i, acc):
            at = pl.ds(pl.multiple_of(i * big, big), big)
            w = wide(w_ref[at, :])
            tile = jnp.where(w > 0, w * jnp.exp(scores[at, :] - top), 0.0)
            return acc + jnp.sum(tile.reshape(big // 8, 8, cols), axis=0)

        acc = lax.fori_loop(0, targets // big, summed, jnp.zeros((8, cols), F32), unroll=UNROLL_A)
        out_ref[0:1, :] = top
        out_ref[1:2, :] = jnp.sum(acc, axis=0, keepdims=True)

    return call(
        body,
        "negative_stats",
        (steps,),
        0,
        [
            pl.BlockSpec((2, width, count), lambda p: (p, 0, 0)),
            full((targets, width)),
            full((targets, 128)),
        ],
        pl.BlockSpec((2, cols), lambda p: (0, p)),
        jax.ShapeDtypeStruct((2, groups * count), F32),
        [pltpu.VMEM((targets, cols), F32)],
    )(src_all, table, times)


def pair_push(src_all, table, stats, counts):
    groups, width, count = src_all.shape
    targets = table.shape[0]
    cols = 2 * count
    steps = groups // 2
    def body(s_ref, t_ref, st_ref, n_ref, nq_ref, soft_ref, q_ref, scores, mz):
        p = pl.program_id(0)

        @pl.when(p == 0)
        def _():
            tops = st_ref[:, 0, :]
            top = jnp.max(tops, axis=0, keepdims=True)
            mz[0:1, :] = top
            mz[1:2, :] = jnp.sum(st_ref[:, 1, :] * jnp.exp(tops - top), axis=0, keepdims=True)

        scores[...] = nn(t_ref[...], pair_of(s_ref))
        lanes = pl.ds(pl.multiple_of(p * cols, cols), cols)
        top = jnp.broadcast_to(mz[0:1, lanes], (TILE, cols))
        total = jnp.broadcast_to(mz[1:2, lanes], (TILE, cols))
        inverse = 1.0 / total

        def tile(i, acc):
            at = pl.ds(pl.multiple_of(i * TILE, TILE), TILE)
            d = scores[at, :] - top
            x = jnp.exp(-jnp.abs(d))
            above = d > 0
            e1 = jnp.where(above, 1.0, x)
            e2 = total * jnp.where(above, x, 1.0)
            nq = n_ref[0, at, :].astype(F32) * (e2 / (e1 + e2))
            nq_ref[0, at, :] = nq.astype(BF)
            soft_ref[0, at, :] = (e1 * inverse).astype(BF)
            return acc + nq

        acc = lax.fori_loop(
            0, targets // TILE, tile, jnp.zeros((TILE, cols), F32), unroll=UNROLL_B
        )
        q_ref[...] = jnp.sum(acc, axis=0, keepdims=True)

    block = pl.BlockSpec((1, targets, cols), lambda p: (p, 0, 0))
    return call(
        body,
        "pair_push",
        (steps,),
        0,
        [
            pl.BlockSpec((2, width, count), lambda p: (p, 0, 0)),
            full((targets, width)),
            full(stats.shape),
            block,
        ],
        [block, block, pl.BlockSpec((1, cols), lambda p: (0, p))],
        [
            jax.ShapeDtypeStruct((steps, targets, cols), BF),
            jax.ShapeDtypeStruct((steps, targets, cols), BF),
            jax.ShapeDtypeStruct((1, groups * count), F32),
        ],
        [
            pltpu.VMEM((targets, cols), F32),
            pltpu.VMEM((2, groups * count), F32),
        ],
    )(src_all, table, stats, counts)


def source_push(nq, soft, q_all, times, table_bf):
    steps, targets, cols = nq.shape
    width = table_bf.shape[0]
    groups = q_all.shape[0]

    def body(nq_ref, soft_ref, q_ref, w_ref, t_ref, d_ref, u_ref, q_sum):
        p = pl.program_id(0)

        @pl.when(p == 0)
        def _():
            q_sum[...] = jnp.sum(q_ref[:, 0, :], axis=0, keepdims=True)

        lanes = pl.ds(pl.multiple_of(p * cols, cols), cols)
        q = jnp.broadcast_to(q_sum[0:1, lanes], (TILE, cols))

        def tile(i, carry):
            at = pl.ds(pl.multiple_of(i * TILE, TILE), TILE)
            push = wide(w_ref[at, :]) * (soft_ref[0, at, :].astype(F32) * q)
            d_ref[0, at, :] = (push - nq_ref[0, at, :].astype(F32)).astype(BF)
            return carry

        lax.fori_loop(0, targets // TILE, tile, 0, unroll=UNROLL_C)
        u = nn(t_ref[...], d_ref[0]).astype(BF)
        u_ref[0] = u[:, : cols // 2]
        u_ref[1] = u[:, cols // 2 :]

    block = pl.BlockSpec((1, targets, cols), lambda p: (p, 0, 0))
    return call(
        body,
        "source_push",
        (steps,),
        0,
        [block, block, full(q_all.shape), full((targets, 128)), full((width, targets))],
        [block, pl.BlockSpec((2, width, cols // 2), lambda p: (p, 0, 0))],
        [
            jax.ShapeDtypeStruct((steps, targets, cols), BF),
            jax.ShapeDtypeStruct((groups, width, cols // 2), BF),
        ],
        [pltpu.VMEM((1, steps * cols), F32)],
    )(nq, soft, q_all, times, table_bf)


def target_update(push, src_all, table_t, state):
    steps, targets, cols = push.shape
    width = table_t.shape[0]
    count = src_all.shape[2]

    def body(d_ref, s_ref, t_ref, st_ref, new_ref, nst_ref, nat_ref, bf_ref, acc):
        p = pl.program_id(0)

        @pl.when(p == 0)
        def _():
            acc[...] = jnp.zeros_like(acc)

        acc[...] += nt(pair_of(s_ref), d_ref[0])

        @pl.when(p == steps - 1)
        def _():
            g = acc[...]
            st = st_ref[...] + jnp.sum(g * g, axis=0, keepdims=True) * (1.0 / width)
            nst_ref[...] = st
            new = t_ref[...] - LEARN * g / jnp.sqrt(st)
            new_ref[...] = new
            bf_ref[...] = new.astype(BF)
            nat_ref[...] = new.T.astype(BF)

    return call(
        body,
        "target_update",
        (steps,),
        0,
        [
            pl.BlockSpec((1, targets, cols), lambda p: (p, 0, 0)),
            pl.BlockSpec((2, width, count), lambda p: (p, 0, 0)),
            full((width, targets)),
            full((1, targets)),
        ],
        [
            full((width, targets)),
            full((1, targets)),
            full((targets, width)),
            full((width, targets)),
        ],
        [
            jax.ShapeDtypeStruct((width, targets), F32),
            jax.ShapeDtypeStruct((1, targets), F32),
            jax.ShapeDtypeStruct((targets, width), BF),
            jax.ShapeDtypeStruct((width, targets), BF),
        ],
        [pltpu.VMEM((width, targets), F32)],
    )(push, src_all, table_t, state)


def source_update(parts, pack):
    groups, width, count = parts.shape

    def body(u_ref, pack_ref, new_ref, bf_ref):
        g = u_ref[0].astype(F32)
        for k in range(1, groups):
            g = g + u_ref[k].astype(F32)
        st = pack_ref[width : width + 1, :] + jnp.sum(g * g, axis=0, keepdims=True) * (1.0 / width)
        new = pack_ref[:width, :] - LEARN * g / jnp.sqrt(st)
        new_ref[:width, :] = new
        bf_ref[...] = new.astype(BF)
        new_ref[width:, :] = jnp.broadcast_to(st, (8, count))

    return call(
        body,
        "source_update",
        (1,),
        0,
        [full(parts.shape), full(pack.shape)],
        [full(pack.shape), full((width, count))],
        [jax.ShapeDtypeStruct(pack.shape, F32), jax.ShapeDtypeStruct((width, count), BF)],
    )(parts, pack)


def slot_holding(sched_row, wanted):
    slots = jnp.arange(sched_row.shape[0], dtype=I32)
    return jnp.sum(slots * (sched_row[None, :] == wanted[:, None]).astype(I32), axis=1)


def shards(
    src_table,
    src_state,
    tgt_table,
    tgt_state,
    pair_source,
    pair_owner,
    pair_offset,
    negatives,
    plan,
):
    my_dom = lax.axis_index("dom")
    groups = lax.axis_size("grp")
    count, width = src_table.shape
    targets = tgt_table.shape[0]
    rounds, doms = plan.shape
    base = (lax.axis_index("grp") * targets).astype(I32).reshape(1)

    lanes = -(-negatives.shape[1] // 128) * 128
    negs = jnp.pad(negatives, ((0, 0), (0, lanes - negatives.shape[1])), constant_values=-1)
    words, times = prepare(
        base, pair_source, pair_owner[:, :, 0], pair_offset, negs, groups, targets
    )
    words = swap_blocks(words)

    words = words.transpose(1, 0, 2).reshape(rounds, groups // 2, 1, -1)

    here = jnp.arange(doms, dtype=I32)
    src = src_table.T.astype(BF)
    pack = jnp.concatenate(
        [src_table.T, jnp.broadcast_to(src_state[None, :], (8, count))], axis=0
    )
    table_t = tgt_table.T
    state = tgt_state[None, :]
    table, table_bf = both_ways(table_t)
    want = plan[0]
    for r in range(rounds):
        src = dom_fetch(src, want, my_dom)
        pack = dom_fetch(pack, want, my_dom)
        if r == 0:
            src, table, table_bf = lax.optimization_barrier((src, table, table_bf))
        src_all = spread(src)
        stats = spread(negative_stats(src_all, table, times))
        counts = pair_counts(words[r], count, targets)
        nq, soft, q = pair_push(src_all, table, stats, counts)
        q_all = spread(q)
        push, parts = source_push(nq, soft, q_all, times, table_bf)
        parts = swap_blocks(parts)
        pack, src = source_update(parts, pack)
        table_t, state, table, table_bf = target_update(push, src_all, table_t, state)
        want = slot_holding(plan[r], plan[r + 1] if r + 1 < rounds else here)
    pack = dom_fetch(pack, want, my_dom)
    return (pack[:width].T, pack[width], table_t.T, state[0])


def solution(mesh):
    both = ("dom", "grp")
    return jax.shard_map(
        shards,
        mesh=mesh,
        in_specs=(
            P(both, None),
            P(both),
            P(both, None),
            P(both),
            P(None, both),
            P(None, both, None),
            P(None, both),
            P("dom", None),
            P(),
        ),
        out_specs=(P(both, None), P(both), P(both, None), P(both)),
        check_vma=False,
    )
```
